32 devices in a mesh: gx: 8 (over y, x, core), gy: 4 (over z).
Axes of the slice: x: 2, y: 2, z: 4, core: 2. Of those that a mesh axis runs over, the one named last changes fastest.
Arguments:
- fractions: float32 [8, 4, 3, 1024], P('gx', 'gy'), may hold values from 0 to 1
- velocity: float32 [8, 4, 3, 1024], P('gx', 'gy'), may hold values from -4 to 4
- drag_rate: float32 [8, 4, 1024], P('gx', 'gy'), may hold values from 0.5 to 4
- volume: float32 [8, 4, 1024], P('gx', 'gy'), may hold values from 0.25 to 1
- owner: int32 [8, 4, 1024, 1], P('gx', 'gy'), may hold values from 0 to 31, as said below
- element: int32 [8, 4, 1024], P('gx', 'gy'), may hold values from 0 to 31
- coords: int32 [8, 4, 3, 1024], P('gx', 'gy'), may hold values from 0 to 63
- fluid: bfloat16 [8, 4, 32, 6, 512], P('gx', 'gy'), may hold values from -4 to 4
Outputs:
- particle_force: float32 [8, 4, 3, 1024], P('gx', 'gy')
- bin_field: float32 [4, 128, 64, 512], P(None, 'gx', 'gy')
The draws below stay inside these ranges and needn't reach their ends.
Inputs may be any that keep to these rules, and one draw needn't show every extreme that they name: owner names a device as its gx index times the number of gy indices plus its gy index: the particle's own device or one whose gx and gy indices each differ from it by at most one (no wrap). A particle owned by a device with gx index one lower has first fraction below 0.2, one higher at least 0.8, the same gx index from 0.2 to 0.8; likewise for gy and the second fraction. Among one device's 1024 particles at most 64 have any one other device as owner, and in every device exactly 64 have one of them.
All inputs are finite; a program needn't handle non-finite values.
Results may differ from the reference program's by a relative error of at most 0.00099.
Values may be sent and summed in bfloat16 or wider, within the bound.
No kernel may reach another device: no remote copies, remote signals or barrier semaphores. Data moves between devices by JAX's collectives and lax.ppermute only.
A program may use at most 64 MiB of HBM per device.

```python
import math
import jax
import jax.numpy as jnp
import numpy as np
from jax import lax

P_DEV = 1024
E_DEV = 32
BINS_THIRD_AXIS = 512
BX = 16
BY = 16
MARGIN = 4
QUANT = 64
CAP = 64
N_GX = 8
N_GY = 4


def neighbour_codes(key):
    base = jax.random.fold_in(key, 7301)
    count_key, order_key = jax.random.split(base)
    grid_i = jnp.arange(N_GX, dtype=jnp.int32)[:, None, None]
    grid_j = jnp.arange(N_GY, dtype=jnp.int32)[None, :, None]
    offsets = jnp.arange(9, dtype=jnp.int32)[None, None, :]
    step_x = offsets // 3 - 1
    step_y = offsets % 3 - 1
    valid = (grid_i + step_x >= 0) & (grid_i + step_x < N_GX) & (grid_j + step_y >= 0) & (grid_j + step_y < N_GY) & (offsets != 4)
    counts = jax.random.randint(count_key, (N_GX, N_GY, 9), 1, CAP + 1).astype(jnp.int32)
    leading = valid & (jnp.cumsum(valid.astype(jnp.int32), axis=2) == 1)
    counts = jnp.where(leading, CAP, counts)
    counts = jnp.where(valid, counts, 0)
    remainder = P_DEV - jnp.sum(counts, axis=2, keepdims=True)
    counts = jnp.where(offsets == 4, remainder, counts)
    bounds = jnp.cumsum(counts, axis=2)
    rows = jnp.arange(P_DEV, dtype=jnp.int32)[None, None, :, None]
    sorted_codes = jnp.sum((rows >= bounds[:, :, None, :]).astype(jnp.int32), axis=3)
    keys = jax.random.split(order_key, N_GX * N_GY)

    def shuffle(single):
        return jax.random.permutation(single, P_DEV)
    orders = jax.vmap(shuffle)(keys).reshape(N_GX, N_GY, P_DEV).astype(jnp.int32)
    return jnp.take_along_axis(sorted_codes, orders, axis=2)


def draw_owner(key, part):
    codes = neighbour_codes(key)
    grid_i = jnp.arange(N_GX, dtype=jnp.int32)[:, None, None]
    grid_j = jnp.arange(N_GY, dtype=jnp.int32)[None, :, None]
    owner = (grid_i + codes // 3 - 1) * N_GY + grid_j + codes % 3 - 1
    return owner.reshape(N_GX, N_GY, P_DEV, 1).astype(jnp.int32)


def edge_fraction(steps, uniform_part):
    return jnp.where(steps < 0, 0.2 * uniform_part, jnp.where(steps > 0, 0.8 + 0.2 * uniform_part, 0.2 + 0.6 * uniform_part))


def draw_fractions(key, part):
    codes = neighbour_codes(key)
    step_x = codes // 3 - 1
    step_y = codes % 3 - 1
    uniform_all = jax.random.uniform(jax.random.fold_in(key, 7411), (N_GX, N_GY, 3, P_DEV), jnp.float32)
    jitter_all = jax.random.uniform(jax.random.fold_in(key, 7523), (N_GX, N_GY, 3, P_DEV), jnp.float32, -1.0, 1.0)
    cluster = jax.random.bernoulli(jax.random.fold_in(key, 7639), 0.5, (N_GX, N_GY, P_DEV))
    depth_centre = jax.random.uniform(jax.random.fold_in(key, 7757), (), jnp.float32, 0.25, 0.75)
    near_centre = 0.02
    far_centre = 0.065
    spread_x = 0.015
    edge_offset = jnp.where(cluster, far_centre, near_centre) + spread_x * jitter_all[:, :, 0]
    along_first = jnp.where(step_x < 0, edge_offset, jnp.where(step_x > 0, 1.0 - edge_offset, 0.2 + 0.6 * uniform_all[:, :, 0]))
    lane_value = 0.5 + 0.4 * step_y.astype(jnp.float32) + 0.015 * jitter_all[:, :, 1]
    along_second = jnp.where(step_x != 0, lane_value, edge_fraction(step_y, uniform_all[:, :, 1]))
    depth_value = depth_centre + 0.1 * BX / BINS_THIRD_AXIS * jitter_all[:, :, 2]
    along_third = jnp.where(step_x != 0, depth_value, uniform_all[:, :, 2])
    stacked = jnp.stack([along_first, along_second, along_third], axis=2)
    return jnp.clip(stacked, 0.0, 1.0).astype(jnp.float32)


def with_ends(array, stream_key, least, high):
    spot = [jax.random.randint(jax.random.fold_in(stream_key, axis), (), 0, length) for axis, length in enumerate(array.shape)]
    longest = array.shape.index(max(array.shape))
    next_to = spot[:longest] + [(spot[longest] + 1) % array.shape[longest]] + spot[longest + 1:]
    return array.at[tuple(spot)].set(least).at[tuple(next_to)].set(high)


def steps_of(stream_key, extent, cuts, smallest, high):
    def one(axis_at, shards_of):
        steps = jax.random.uniform(jax.random.fold_in(jax.random.fold_in(stream_key, 6), axis_at), (shards_of,), jnp.float32, smallest / len(cuts), high / len(cuts))
        return jnp.repeat(jnp.exp(steps), extent[axis_at] // shards_of).reshape((-1,) + (1,) * (len(extent) - axis_at - 1))

    factor_of = one(*cuts[0])
    for cut in cuts[1:]:
        factor_of = factor_of * one(*cut)
    return factor_of


def noise(stream_key, dims, scale, limit, cuts=(), held_as=jnp.bfloat16):
    values = scale * jax.random.normal(stream_key, dims, jnp.float32)
    if cuts:
        values = values * steps_of(stream_key, dims, cuts, -0.22, 0.18)
    return jnp.clip(values, -limit, limit).astype(held_as)


def setup_inputs(seed: int = 0) -> dict:
    key_list = jax.random.split(jax.random.key(seed), 9)
    fractions = draw_fractions(jax.random.fold_in(key_list[8], 71), 0)
    velocity = noise(key_list[1], (N_GX, N_GY, 3, P_DEV), 0.25, 4.0, ((0, 8), (1, 4)), jnp.float32)
    drag_rate = jnp.clip(jnp.exp(math.log(4.0) - 2.0794415 * jax.random.uniform(key_list[2], (N_GX, N_GY, P_DEV), jnp.float32) ** steps_of(key_list[2], (N_GX, N_GY, P_DEV), ((0, 8), (1, 4)), -0.2, 0.2)), 0.5, 4.0)
    volume = jnp.clip(jnp.exp(math.log(1.0) - 1.3862944 * jax.random.uniform(key_list[3], (N_GX, N_GY, P_DEV), jnp.float32) ** steps_of(key_list[3], (N_GX, N_GY, P_DEV), ((0, 8), (1, 4)), -0.2, 0.2)), 0.25, 1.0)
    owner = draw_owner(jax.random.fold_in(key_list[8], 71), 0)
    element = with_ends(jax.random.randint(key_list[5], (N_GX, N_GY, P_DEV), 0, E_DEV), jax.random.fold_in(key_list[5], 1), 0, E_DEV - 1).astype(jnp.int32)
    coords = with_ends(jax.random.randint(key_list[6], (N_GX, N_GY, 3, P_DEV), 0, QUANT), jax.random.fold_in(key_list[6], 1), 0, QUANT - 1).astype(jnp.int32)
    fluid = noise(key_list[7], (N_GX, N_GY, E_DEV, 6, 512), 0.25, 4.0, ((0, 8), (1, 4)))
    return dict(fractions=fractions, velocity=velocity, drag_rate=drag_rate, volume=volume, owner=owner, element=element, coords=coords, fluid=fluid)


GLL_NODES = (-1.0, -0.8717401485096066, -0.5917001814331423, -0.2092992179024789,
             0.2092992179024789, 0.5917001814331423, 0.8717401485096066, 1.0)
STIFFNESS = 0.5
PAIR_WIDTH = 0.3
FILTER_BINS = 3.0


def basis_table(levels):
    points = -1.0 + (2.0 * np.arange(levels) + 1.0) / levels
    lagrange = np.ones((levels, 8))
    for node_a in range(8):
        for node_b in range(8):
            if node_b != node_a:
                lagrange[:, node_a] *= (points - GLL_NODES[node_b]) / (GLL_NODES[node_a] - GLL_NODES[node_b])
    return jnp.asarray(lagrange, dtype=jnp.float32)


def place(fractions, slab_x, slab_y):
    return jnp.stack([slab_x + fractions[0], slab_y + fractions[1], fractions[2] * (BINS_THIRD_AXIS / BX)])


def gaussian_rows(along, centres, deviation):
    distance = along[:, None] - centres[None, :]
    bumps = jnp.exp(-(distance * distance) / (2.0 * deviation * deviation))
    return bumps / jnp.sum(bumps, axis=1, keepdims=True)


def window_spread(positions, loads, slab_x, slab_y, span_x, span_y):
    first_extent = BX + 2 * MARGIN
    second_extent = BY + 2 * MARGIN
    centre_x = slab_x + (jnp.arange(first_extent, dtype=jnp.float32) - MARGIN + 0.5) / BX
    centre_y = slab_y + (jnp.arange(second_extent, dtype=jnp.float32) - MARGIN + 0.5) / BY
    centre_z = (jnp.arange(BINS_THIRD_AXIS, dtype=jnp.float32) + 0.5) / BX
    along_x = gaussian_rows(positions[0], centre_x, FILTER_BINS / BX)[:, span_x[0]:span_x[0] + span_x[1]]
    along_y = gaussian_rows(positions[1], centre_y, FILTER_BINS / BY)[:, span_y[0]:span_y[0] + span_y[1]]
    along_depth = gaussian_rows(positions[2], centre_z, FILTER_BINS / BX).astype(jnp.bfloat16)
    plane = (along_x[:, :, None] * along_y[:, None, :]).reshape(positions.shape[1], span_x[1] * span_y[1])
    scattered_loads = (loads[:, :, None] * plane[None, :, :]).astype(jnp.bfloat16)
    return scattered_loads, along_depth


def pair_forces(own, blocks, present):
    particles = own.shape[1]
    row_count = min(512, particles)
    groups = particles // row_count
    stacked = own.reshape(3, groups, row_count).transpose(1, 0, 2)

    def one_group(subset):
        summed = jnp.zeros((3, row_count), own.dtype)
        for ghost_block, weight in zip(blocks, present):
            offset = subset[:, :, None] - ghost_block[:, None, :]
            closeness = jnp.exp(-jnp.sum(offset * offset, axis=0) / (2.0 * PAIR_WIDTH * PAIR_WIDTH)) * weight
            summed = summed + jnp.sum(offset * closeness[None, :, :], axis=2)
        return summed

    return STIFFNESS * lax.map(one_group, stacked).transpose(1, 0, 2).reshape(3, particles)


def reference(fractions, velocity, drag_rate, volume, owner, element, coords, fluid):
    grid_x = fractions.shape[0]
    grid_y = fractions.shape[1]
    devices = grid_x * grid_y
    lagrange = basis_table(QUANT)
    table = fluid.reshape(devices * E_DEV, 6, 512)

    def interpolate(inputs):
        targets, local_ids, levels = inputs
        picked = table[targets * E_DEV + local_ids].astype(jnp.float32)
        first = lagrange[levels[0]]
        second = lagrange[levels[1]]
        third = lagrange[levels[2]]
        weights = (first[:, :, None, None] * second[:, None, :, None] * third[:, None, None, :]).reshape(-1, 512)
        weights = lax.optimization_barrier(weights.astype(jnp.bfloat16)).astype(jnp.float32)
        return jnp.einsum("pkn,pn->kp", picked, weights).astype(jnp.bfloat16)

    fetched = lax.map(interpolate, (owner.reshape(devices, P_DEV), element.reshape(devices, P_DEV),
                                    coords.reshape(devices, 3, P_DEV)))
    padded = jnp.pad(fractions, ((1, 1), (1, 1), (0, 0), (0, 0)))
    alive_grid = jnp.pad(jnp.ones((grid_x, grid_y), jnp.float32), 1)
    velocity_rows = velocity.reshape(devices, 3, P_DEV)
    drag_rows = drag_rate.reshape(devices, P_DEV)
    volume_rows = volume.reshape(devices, P_DEV)
    first_extent = BX + 2 * MARGIN
    second_extent = BY + 2 * MARGIN
    field = jnp.zeros((4, grid_x * BX + 2 * MARGIN, grid_y * BY + 2 * MARGIN, BINS_THIRD_AXIS), jnp.float32)
    nought = jnp.zeros((), jnp.int32)

    def per_device(field, flat):
        index_x = (flat // grid_y).astype(jnp.int32)
        index_y = (flat % grid_y).astype(jnp.int32)
        slab_x = index_x.astype(jnp.float32)
        slab_y = index_y.astype(jnp.float32)
        nearby = lax.dynamic_slice(padded, (index_x, index_y, nought, nought), (3, 3, 3, P_DEV))
        alive = lax.dynamic_slice(alive_grid, (index_x, index_y), (3, 3))
        blocks = []
        present = []
        for shift_x in (-1, 0, 1):
            for shift_y in (-1, 0, 1):
                blocks.append(place(nearby[1 + shift_x, 1 + shift_y], slab_x + shift_x, slab_y + shift_y))
                present.append(alive[1 + shift_x, 1 + shift_y])
        own = place(nearby[1, 1], slab_x, slab_y)
        pair = pair_forces(own, blocks, present)
        values = fetched[flat].astype(jnp.float32)
        force = drag_rows[flat][None, :] * (values[0:3] - velocity_rows[flat]) - volume_rows[flat][None, :] * values[3:6] + pair
        loads = jnp.concatenate([force, volume_rows[flat][None, :]], axis=0)
        scattered_loads, along_depth = window_spread(own, loads, slab_x, slab_y, (0, first_extent), (0, second_extent))
        scatter_extent = lax.optimization_barrier(scattered_loads).astype(jnp.float32)
        depth_extent = lax.optimization_barrier(along_depth).astype(jnp.float32)
        filter_cube = jnp.einsum("vtn,tl->vnl", scatter_extent, depth_extent).reshape(4, first_extent, second_extent, BINS_THIRD_AXIS)
        corner = (nought, index_x * BX, index_y * BY, nought)
        region = lax.dynamic_slice(field, corner, filter_cube.shape) + filter_cube
        return lax.dynamic_update_slice(field, region, corner), force

    field, forces = lax.scan(per_device, field, jnp.arange(devices, dtype=jnp.int32))
    bin_field = field[:, MARGIN:MARGIN + grid_x * BX, MARGIN:MARGIN + grid_y * BY] * (BX * BY * BINS_THIRD_AXIS / P_DEV)
    return forces.reshape(grid_x, grid_y, 3, P_DEV), bin_field
```

```python
import math
from functools import partial

import jax
import jax.numpy as jnp
import numpy as np
from jax import lax
from jax.experimental import pallas as pl
from jax.experimental.pallas import tpu as pltpu
from jax.sharding import PartitionSpec as P

BX = 16
BY = 16
MARGIN = 4
QUANT = 64
CAP = 64
NODES = 8

GLL_NODES = (
    -1.0,
    -0.8717401485096066,
    -0.5917001814331423,
    -0.2092992179024789,
    0.2092992179024789,
    0.5917001814331423,
    0.8717401485096066,
    1.0,
)
STIFFNESS = 0.5
PAIR_WIDTH = 0.3
FILTER_BINS = 3.0

F32 = jnp.float32
BF16 = jnp.bfloat16
VMEM = pl.BlockSpec(memory_space=pltpu.VMEM)
PAIR_SCALE = math.sqrt(math.log2(math.e)) / PAIR_WIDTH
FILTER_SCALE = math.sqrt(0.5 * math.log2(math.e)) / FILTER_BINS
NEVER = -1e30


def basis_table(levels):
    points = -1.0 + (2.0 * np.arange(levels) + 1.0) / levels
    lagrange = np.ones((levels, NODES))
    for node_a in range(NODES):
        for node_b in range(NODES):
            if node_b != node_a:
                lagrange[:, node_a] *= (points - GLL_NODES[node_b]) / (
                    GLL_NODES[node_a] - GLL_NODES[node_b]
                )
    return lagrange.astype(np.float32)


def split_table():
    table = basis_table(QUANT).T
    parts = []
    for _ in range(3):
        head = table.astype(jnp.bfloat16)
        parts.append(head)
        table = table - head.astype(np.float32)
    return np.concatenate(parts, axis=0)


def split3(values):
    first = values.astype(BF16).astype(F32)
    rest = values - first
    second = rest.astype(BF16).astype(F32)
    return first, second, rest - second


def partner(axis, which):
    index = lax.axis_index(axis)
    step = 1 - 2 * lax.rem(index, 2)
    if which:
        step = -step
    there = index + step
    return step, (there >= 0) & (there < lax.axis_size(axis))


def swap(block, axis, which):
    count = lax.axis_size(axis)
    pairs = [(i, i + 1) for i in range(which, count - 1, 2)]
    return lax.ppermute(block, axis, pairs + [(b, a) for a, b in pairs])


def features(block, step_x, step_y, present, half_depth):
    row = lax.broadcasted_iota(jnp.int32, block.shape, 0)
    scale = jnp.where(row == 2, 2.0 * half_depth * PAIR_SCALE, PAIR_SCALE)
    shift = jnp.where(
        row == 0,
        (step_x.astype(F32) - 0.5) * PAIR_SCALE,
        jnp.where(row == 1, (step_y.astype(F32) - 0.5) * PAIR_SCALE, -half_depth * PAIR_SCALE),
    )
    place = jnp.where(row < 3, block * scale + shift, 0.0)
    norm = -0.5 * jnp.sum(place * place, axis=0, keepdims=True)
    norm = jnp.where(present, norm, NEVER)
    source = jnp.where(row == 3, norm, jnp.where(row == 4, 1.0, place))
    target = jnp.where(row == 3, 1.0, jnp.where(row == 4, norm, place))
    return place, source, target


def target_rows(own, half_depth):
    place, _, target = features(own, jnp.int32(0), jnp.int32(0), True, half_depth)
    a, b, c = split3(target)
    return place, jnp.concatenate([a, b, a, b, c, a], axis=0).astype(BF16)


def depth_centres(depth):
    return (lax.broadcasted_iota(jnp.int32, (1, depth), 1).astype(F32) + 0.5) * FILTER_SCALE


def depth_column(block, depth):
    return jnp.transpose(block[0:8] * (depth * FILTER_SCALE))[:, 2:3]


def depth_rows(column, depth):
    distance = column - depth_centres(depth)
    bumps = jnp.exp2(-(distance * distance))
    return (bumps * (1.0 / jnp.sum(bumps, axis=1, keepdims=True))).astype(BF16)


def pair_block(block, step_x, step_y, present, half_depth, target_ref, total_ref, depth_ref):
    particles = block.shape[1]
    depth = depth_ref.shape[1]
    column = depth_column(block, depth)
    _, source, _ = features(block, step_x, step_y, present, half_depth)
    a, b, c = split3(source)
    rows = jnp.concatenate([a, a, b, b, a, c], axis=0).astype(BF16)
    values = jnp.concatenate([a, b, c, jnp.zeros_like(a)], axis=0).astype(BF16)
    width = min(256, particles)
    for start in range(0, particles, width):
        exponent = lax.dot_general(
            rows,
            target_ref[:, start : start + width],
            (((0,), (0,)), ((), ())),
            preferred_element_type=F32,
        )
        weight = jnp.exp2(exponent)
        high = weight.astype(BF16)
        low = (weight - high.astype(F32)).astype(BF16)
        sums = jnp.dot(values, high, preferred_element_type=F32) + jnp.dot(
            values, low, preferred_element_type=F32
        )
        total_ref[:, start : start + width] += sums[0:8] + sums[8:16] + sums[16:24]
        depth_ref[start : start + width] = depth_rows(column[start : start + width], depth)


def y_steps():
    step_a, has_a = partner("gy", 0)
    step_b, has_b = partner("gy", 1)
    return ((step_a, has_a), (jnp.int32(0), jnp.bool_(True)), (step_b, has_b))


def interpolate(request, table_ref, basis_ref, weight_ref):
    slots = request.shape[1]
    elements = table_ref.shape[0] // 6
    level = lax.broadcasted_iota(jnp.int32, (QUANT, slots), 0).astype(F32)
    factors = []
    for axis in range(3):
        chosen = jnp.where(level == request[1 + axis : 2 + axis], 1.0, 0.0).astype(BF16)
        parts = jnp.dot(basis_ref[...], chosen, preferred_element_type=F32)
        factors.append(parts[0:8] + (parts[8:16] + parts[16:24]))
    for a in range(NODES):
        first = factors[0][a : a + 1] * factors[1]
        for b in range(0, NODES, 2):
            pair = jnp.concatenate(
                [first[b : b + 1] * factors[2], first[b + 1 : b + 2] * factors[2]], axis=0
            )
            start = (a * NODES + b) * NODES
            weight_ref[start : start + 2 * NODES, :slots] = pair.astype(BF16)
    projected = jnp.dot(table_ref[...], weight_ref[:, :slots], preferred_element_type=F32)
    local = lax.broadcasted_iota(jnp.int32, (elements, slots), 0).astype(F32)
    picked = jnp.where(local == request[0:1], 1.0, 0.0)
    rows = [
        jnp.sum(projected[k * elements : (k + 1) * elements] * picked, axis=0, keepdims=True)
        for k in range(6)
    ]
    return jnp.concatenate(rows + [jnp.zeros((2, slots), F32)], axis=0)


def my_flat():
    return (lax.axis_index("gx") * lax.axis_size("gy") + lax.axis_index("gy")).astype(F32)


def pack_kernel(fractions_ref, owner_ref, element_ref, coords_ref, out_ref):
    for k in range(3):
        out_ref[k : k + 1] = fractions_ref[k]
        out_ref[5 + k : 6 + k] = coords_ref[k].astype(F32)
    out_ref[3:4] = owner_ref[...].astype(F32)
    out_ref[4:5] = element_ref[...].astype(F32)


def own_kernel(
    half_depth, own_ref, far_table_ref, far_basis_ref, total_ref, values_ref, depth_ref,
    target_ref, weight_ref, table_ref, basis_ref, arrived,
):
    fetches = [
        pltpu.make_async_copy(far_table_ref, table_ref, arrived.at[0]),
        pltpu.make_async_copy(far_basis_ref, basis_ref, arrived.at[1]),
    ]
    for fetch in fetches:
        fetch.start()
    own = own_ref[...]
    _, target = target_rows(own, half_depth)
    target_ref[...] = target
    total_ref[...] = jnp.zeros_like(total_ref)
    zero = jnp.int32(0)
    pair_block(own, zero, zero, True, half_depth, target_ref, total_ref, depth_ref)
    for fetch in fetches:
        fetch.wait()
    values = interpolate(own[4:8], table_ref, basis_ref, weight_ref)
    values_ref[...] = jnp.where(own[3:4] == my_flat(), values, 0.0).astype(BF16)


def column_kernel(
    half_depth, own_ref, first_ref, second_ref, sum_ref, total_ref, depth_ref, target_ref
):
    _, target = target_rows(own_ref[...], half_depth)
    target_ref[...] = target
    total_ref[...] = sum_ref[...]
    steps = y_steps()
    zero = jnp.int32(0)
    for n, (ref, (step, present)) in enumerate(((first_ref, steps[0]), (second_ref, steps[2]))):
        pair_block(ref[...], zero, step, present, half_depth, target_ref, total_ref, depth_ref.at[n])


def side_kernel(
    which, half_depth, own_ref, blocks_ref, sum_ref, total_ref, depth_ref, target_ref
):
    _, target = target_rows(own_ref[...], half_depth)
    target_ref[...] = target
    total_ref[...] = sum_ref[...]
    step_x, has_x = partner("gx", which)
    for k, (step, present) in enumerate(y_steps()):
        pair_block(
            blocks_ref[k], step_x, step, present & has_x, half_depth, target_ref, total_ref,
            depth_ref.at[k],
        )


def serve_kernel(
    za_ref, zb_ref, xa_ref, xb_ref, table_ref, basis_ref,
    zout_ref, xaout_ref, xbout_ref, chosen_ref, weight_ref,
):
    particles = za_ref.shape[1]
    steps = y_steps()
    _, has_a = partner("gx", 0)
    _, has_b = partner("gx", 1)
    blocks = [(za_ref[...], steps[0][1], (zout_ref, 0)), (zb_ref[...], steps[2][1], (zout_ref, 1))]
    for ref, out, has in ((xa_ref, xaout_ref, has_a), (xb_ref, xbout_ref, has_b)):
        for k in range(3):
            blocks.append((ref[k], steps[k][1] & has, (out, k)))
    me = my_flat()
    mask = jnp.concatenate(
        [jnp.where((b[3:4] == me) & present, 1.0, 0.0) for b, present, _ in blocks], axis=0
    )
    lanes = 128
    chunks = particles // lanes
    upper = jnp.where(
        lax.broadcasted_iota(jnp.int32, (lanes, lanes), 0)
        < lax.broadcasted_iota(jnp.int32, (lanes, lanes), 1),
        1.0,
        0.0,
    ).astype(BF16)
    stacked = jnp.concatenate([mask[:, j * lanes : (j + 1) * lanes] for j in range(chunks)], axis=0)
    inside = jnp.dot(stacked.astype(BF16), upper, preferred_element_type=F32)
    counts = jnp.sum(stacked, axis=1, keepdims=True)
    before = jnp.zeros((8, 1), F32)
    ranks = []
    for j in range(chunks):
        ranks.append(inside[8 * j : 8 * j + 8] + before)
        before = before + counts[8 * j : 8 * j + 8]
    rank = jnp.concatenate(ranks, axis=1)
    slot = lax.broadcasted_iota(jnp.int32, (2 * CAP, particles), 0).astype(F32)
    requests = []
    for pair in range(4):
        part = jnp.zeros((8, 2 * CAP), F32)
        for half in range(2):
            b = 2 * pair + half
            place = jnp.where(mask[b : b + 1] > 0.0, rank[b : b + 1] + half * CAP, -1.0)
            chosen = jnp.where(slot == place, 1.0, 0.0).astype(BF16)
            chosen_ref[b] = chosen
            part = part + lax.dot_general(
                blocks[b][0].astype(BF16), chosen, (((1,), (1,)), ((), ())), preferred_element_type=F32
            )
        requests.append(part)
    request = jnp.concatenate(requests, axis=1)
    values = interpolate(request[4:8], table_ref, basis_ref, weight_ref).astype(BF16)
    for b, (_, _, (out, k)) in enumerate(blocks):
        reply = values[:, (b // 2) * 2 * CAP : (b // 2 + 1) * 2 * CAP]
        out[k] = jnp.dot(reply, chosen_ref[b], preferred_element_type=F32).astype(BF16)


def join_kernel(own_ref, z_ref, xa_ref, xb_ref, mid_ref, za_ref, zb_ref):
    za_ref[...] = z_ref[0] + (xa_ref[0] + xb_ref[0])
    mid_ref[...] = own_ref[...] + (xa_ref[1] + xb_ref[1])
    zb_ref[...] = z_ref[1] + (xa_ref[2] + xb_ref[2])


def force_kernel(
    half_depth, own_ref, mid_ref, za_ref, zb_ref, total_ref, velocity_ref, drag_ref, volume_ref,
    force_ref, loads_ref,
):
    place, _, _ = features(own_ref[...], jnp.int32(0), jnp.int32(0), True, half_depth)
    total = total_ref[...]
    pair = (STIFFNESS / PAIR_SCALE) * (place[0:3] * total[4:5] - total[0:3])
    fetched = (mid_ref[...] + (za_ref[...] + zb_ref[...])).astype(F32)
    for k in range(3):
        force = (
            drag_ref[...] * (fetched[k : k + 1] - velocity_ref[k])
            - volume_ref[...] * fetched[3 + k : 4 + k]
            + pair[k : k + 1]
        )
        force_ref[k] = force
        loads_ref[k : k + 1] = force
    loads_ref[3:4] = volume_ref[...]


def side_weights(fraction_row, bins, first, count, rows, low):
    particles = fraction_row.shape[1]
    extent = bins + 2 * MARGIN
    along = fraction_row * (bins * FILTER_SCALE)
    index = lax.broadcasted_iota(jnp.int32, (extent, particles), 0).astype(F32)
    distance = along - (index - (MARGIN - 0.5)) * FILTER_SCALE
    inverse = 1.0 / jnp.sum(jnp.exp2(-(distance * distance)), axis=0, keepdims=True)
    row = lax.broadcasted_iota(jnp.int32, (rows, particles), 0)
    here = row.astype(F32) + first.astype(F32)
    distance = along - (here - (MARGIN - 0.5)) * FILTER_SCALE
    bumps = jnp.exp2(-(distance * distance)) * inverse
    return jnp.where((row >= low) & (row < low + count), bumps, 0.0)


def cross_axis(step, bins):
    return jnp.where(step < 0, bins + MARGIN, 0), jnp.where(step < 0, 0, bins - MARGIN)


def x_part(block, step):
    first, to = cross_axis(step, BX)
    return side_weights(block[0:1], BX, first, MARGIN, 8, 0), to


def y_part(block, step):
    first, _ = cross_axis(step, BY)
    low = jnp.where(step < 0, 0, MARGIN)
    return side_weights(block[1:2], BY, first - low, MARGIN, 8, low), jnp.where(step < 0, 0, BY - 8)


def whole_part(row, bins):
    return side_weights(row, bins, jnp.int32(MARGIN), bins, bins, 0)


def spread_rows(along_x, count_x, along_y, load, spread_ref):
    rows = along_y.shape[0]
    group = max(1, 16 // rows)
    for a in range(0, count_x, group):
        parts = [(along_x[a + i : a + i + 1] * along_y) * load for i in range(group)]
        part = parts[0] if group == 1 else jnp.concatenate(parts, axis=0)
        spread_ref[a * rows : (a + group) * rows] = part.astype(BF16)


def spread_product(along_x, count_x, along_y, load, depth, spread_ref):
    rows = along_y.shape[0]
    spread_rows(along_x, count_x, along_y, load, spread_ref)
    piece = jnp.dot(spread_ref[: count_x * rows], depth, preferred_element_type=F32)
    return piece.reshape(count_x, rows, piece.shape[1])


def filter_own_kernel(scale, own_ref, loads_ref, depth_ref, out_ref, spread_ref):
    own = own_ref[...]
    depth = depth_ref[...]
    along_x = whole_part(own[0:1], BX)
    along_y = whole_part(own[1:2], BY)
    for c in range(4):
        out_ref[c] = spread_product(
            along_x, BX, along_y, loads_ref[c : c + 1] * scale, depth, spread_ref
        )


def filter_x_kernel(scale, xa_ref, xb_ref, la_ref, lb_ref, da_ref, db_ref, out_ref, spread_ref):
    for which, (ref, loads, depth_ref) in enumerate(
        ((xa_ref, la_ref, da_ref), (xb_ref, lb_ref, db_ref))
    ):
        block = ref[1]
        step, _ = partner("gx", which)
        depth = depth_ref[1]
        along_x, _ = x_part(block, step)
        along_y = whole_part(block[1:2], BY)
        for c in range(4):
            out_ref[which, c] = spread_product(
                along_x, MARGIN, along_y, loads[c : c + 1] * scale, depth, spread_ref
            )


def rest_blocks(za_ref, zb_ref, xa_ref, xb_ref):
    for side in range(2):
        for column in range(3):
            if column == 1:
                yield side, column, (za_ref, zb_ref)[side][...]
            else:
                yield side, column, (xa_ref, xb_ref)[column // 2][2 * side]


def filter_rest_kernel(
    scale, za_ref, zb_ref, xa_ref, xb_ref, la_ref, lb_ref, dz_ref, da_ref, db_ref, side_ref,
    field_ref, out_ref, x_ref, y_ref, spread_ref,
):
    c = pl.program_id(0)
    steps = y_steps()
    steps = (steps[0][0], steps[2][0])

    @pl.when(c == 0)
    def _():
        for side, column, block in rest_blocks(za_ref, zb_ref, xa_ref, xb_ref):
            n = 3 * side + column
            y_ref[n] = y_part(block, steps[side])[0]
            if column == 1:
                x_ref[n] = whole_part(block[0:1], BX)
            else:
                x_ref[n, 0:8] = x_part(block, partner("gx", column // 2)[0])[0]

    out_ref[...] = field_ref[...]
    for which in range(2):
        _, to_x = cross_axis(partner("gx", which)[0], BX)
        out_ref[0, pl.ds(to_x, MARGIN)] += side_ref[which, 0]
    for side, loads in enumerate((la_ref, lb_ref)):
        to_y = pl.multiple_of(jnp.where(steps[side] < 0, 0, BY - 8), 8)
        for column in range(3):
            n = 3 * side + column
            if column == 1:
                to_x, count = 0, BX
            else:
                _, to_x = cross_axis(partner("gx", column // 2)[0], BX)
                count = MARGIN
            load = loads[column, pl.ds(c, 1)] * scale
            depth = dz_ref[side] if column == 1 else (da_ref, db_ref)[column // 2][2 * side]
            piece = spread_product(x_ref[n], count, y_ref[n], load, depth, spread_ref)
            out_ref[0, pl.ds(to_x, count), pl.ds(to_y, 8)] += piece


def call(kernel, shapes, args, scratch=(), flops=0, name=None, mib=12, far=()):
    many = isinstance(shapes, list)
    return pl.pallas_call(
        kernel,
        out_shape=shapes,
        in_specs=[
            pl.BlockSpec(memory_space=pltpu.HBM) if i in far else VMEM for i in range(len(args))
        ],
        out_specs=[VMEM] * len(shapes) if many else VMEM,
        scratch_shapes=list(scratch),
        cost_estimate=pl.CostEstimate(flops=flops, bytes_accessed=1 << 16, transcendentals=0),
        compiler_params=pltpu.CompilerParams(vmem_limit_bytes=mib << 20),
        name=name,
    )(*args)


def body(fractions, velocity, drag_rate, volume, owner, element, coords, fluid):
    particles = fractions.shape[3]
    elements = fluid.shape[2]
    depth = 512
    half_depth = 0.5 * depth / BX
    table = fluid.reshape(elements, 6, fluid.shape[4]).transpose(1, 0, 2)
    table = table.reshape(6 * elements, fluid.shape[4])
    basis = jnp.asarray(split_table())
    row = (1, particles)
    planes = (3, 1, particles)
    block = jax.ShapeDtypeStruct((8, particles), F32)
    reply = jax.ShapeDtypeStruct((8, particles), BF16)
    target = pltpu.VMEM((48, particles), BF16)
    weights = pltpu.VMEM((fluid.shape[4], max(particles, 8 * CAP)), BF16)
    cost = particles * particles * 1000

    own = call(
        pack_kernel,
        block,
        (fractions.reshape(planes), owner.reshape(row), element.reshape(row), coords.reshape(planes)),
        flops=1000,
        name="pack",
        mib=60,
    )
    zb = swap(own, "gy", 1)
    za = swap(own, "gy", 0)
    def depths(*lead):
        return jax.ShapeDtypeStruct((*lead, particles, depth), BF16)

    total, values, d_own = call(
        partial(own_kernel, half_depth),
        [block, reply, depths()],
        (own, table, basis),
        (target, weights, pltpu.VMEM(table.shape, BF16), pltpu.VMEM(basis.shape, BF16), pltpu.SemaphoreType.DMA((2,))),
        flops=2 * cost,
        name="own",
        far=(1, 2),
    )
    column = jnp.stack([za, own, zb])
    xb = swap(column, "gx", 1)
    xa = swap(column, "gx", 0)
    total, d_z = call(
        partial(column_kernel, half_depth),
        [block, depths(2)],
        (own, za, zb, total),
        (target,),
        flops=2 * cost,
        name="column",
    )
    reply3 = jax.ShapeDtypeStruct((3, 8, particles), BF16)
    reply2 = jax.ShapeDtypeStruct((2, 8, particles), BF16)
    z_out, xa_out, xb_out = call(
        serve_kernel,
        [reply2, reply3, reply3],
        (za, zb, xa, xb, table, basis),
        (pltpu.VMEM((8, 2 * CAP, particles), BF16), weights),
        flops=2 * cost,
        name="serve",
        mib=12,
    )
    xb_in = swap(xb_out, "gx", 1)
    xa_in = swap(xa_out, "gx", 0)
    total, d_a = call(
        partial(side_kernel, 0, half_depth),
        [block, depths(3)],
        (own, xa, total),
        (target,),
        flops=3 * cost,
        name="side_a",
    )
    mid, za_out, zb_out = call(
        join_kernel, [reply] * 3, (values, z_out, xa_in, xb_in), flops=1000, name="join"
    )
    zb_in = swap(zb_out, "gy", 1)
    za_in = swap(za_out, "gy", 0)
    total, d_b = call(
        partial(side_kernel, 1, half_depth),
        [block, depths(3)],
        (own, xb, total),
        (target,),
        flops=3 * cost,
        name="side_b",
    )
    force, loads = call(
        partial(force_kernel, half_depth),
        [jax.ShapeDtypeStruct(planes, F32), jax.ShapeDtypeStruct((4, particles), F32)],
        (
            own,
            mid,
            za_in,
            zb_in,
            total,
            velocity.reshape(planes),
            drag_rate.reshape(row),
            volume.reshape(row),
        ),
        flops=1000,
        name="force",
    )
    lb = swap(loads, "gx", 1)
    la = swap(loads, "gx", 0)
    scale = BX * BY * depth / particles
    spread = pltpu.VMEM((BX * BY, particles), BF16)
    field = call(
        partial(filter_own_kernel, scale),
        jax.ShapeDtypeStruct((4, BX, BY, depth), F32),
        (own, loads, d_own),
        (spread,),
        flops=2 * cost,
        name="filter_own",
        mib=16,
    )
    load_row = jnp.stack([la, loads, lb])
    lzb = swap(load_row, "gy", 1)
    lza = swap(load_row, "gy", 0)
    sides = call(
        partial(filter_x_kernel, scale),
        jax.ShapeDtypeStruct((2, 4, MARGIN, BY, depth), F32),
        (xa, xb, la, lb, d_a, d_b),
        (spread,),
        flops=2 * cost,
        name="filter_x",
        mib=16,
    )
    field = pl.pallas_call(
        partial(filter_rest_kernel, scale),
        grid=(4,),
        out_shape=jax.ShapeDtypeStruct((4, BX, BY, depth), F32),
        in_specs=[VMEM] * 9
        + [
            pl.BlockSpec((2, 1, MARGIN, BY, depth), lambda c: (0, c, 0, 0, 0)),
            pl.BlockSpec((1, BX, BY, depth), lambda c: (c, 0, 0, 0)),
        ],
        out_specs=pl.BlockSpec((1, BX, BY, depth), lambda c: (c, 0, 0, 0)),
        scratch_shapes=[
            pltpu.VMEM((6, BX, particles), F32),
            pltpu.VMEM((6, 8, particles), F32),
            spread,
        ],
        cost_estimate=pl.CostEstimate(flops=4 * cost, bytes_accessed=1 << 16, transcendentals=0),
        compiler_params=pltpu.CompilerParams(vmem_limit_bytes=16 << 20),
        name="filter_rest",
    )(za, zb, xa, xb, lza, lzb, d_z, d_a, d_b, sides, field)
    return (force.reshape(1, 1, 3, particles), field)


def solution(mesh):
    return jax.shard_map(
        body,
        mesh=mesh,
        in_specs=(
            P("gx", "gy", None, None),
            P("gx", "gy", None, None),
            P("gx", "gy", None),
            P("gx", "gy", None),
            P("gx", "gy", None, None),
            P("gx", "gy", None),
            P("gx", "gy", None, None),
            P("gx", "gy", None, None, None),
        ),
        out_specs=(P("gx", "gy", None, None), P(None, "gx", "gy", None)),
        check_vma=False,
    )
```

```python
import math
from functools import partial

import jax
import jax.numpy as jnp
import numpy as np
from jax import lax
from jax.experimental import pallas as pl
from jax.experimental.pallas import tpu as pltpu
from jax.sharding import PartitionSpec as P

BX = 16
BY = 16
MARGIN = 4
QUANT = 64
CAP = 64
NODES = 8

GLL_NODES = (
    -1.0,
    -0.8717401485096066,
    -0.5917001814331423,
    -0.2092992179024789,
    0.2092992179024789,
    0.5917001814331423,
    0.8717401485096066,
    1.0,
)
STIFFNESS = 0.5
PAIR_WIDTH = 0.3
FILTER_BINS = 3.0

F32 = jnp.float32
BF16 = jnp.bfloat16
VMEM = pl.BlockSpec(memory_space=pltpu.VMEM)
PAIR_SCALE = math.sqrt(math.log2(math.e)) / PAIR_WIDTH
FILTER_SCALE = math.sqrt(0.5 * math.log2(math.e)) / FILTER_BINS
NEVER = -1e30


def basis_table(levels):
    points = -1.0 + (2.0 * np.arange(levels) + 1.0) / levels
    lagrange = np.ones((levels, NODES))
    for node_a in range(NODES):
        for node_b in range(NODES):
            if node_b != node_a:
                lagrange[:, node_a] *= (points - GLL_NODES[node_b]) / (
                    GLL_NODES[node_a] - GLL_NODES[node_b]
                )
    return lagrange.astype(np.float32)


def split_table():
    table = basis_table(QUANT).T
    parts = []
    for _ in range(3):
        head = table.astype(jnp.bfloat16)
        parts.append(head)
        table = table - head.astype(np.float32)
    return np.concatenate(parts, axis=0)


def split3(values):
    first = values.astype(BF16).astype(F32)
    rest = values - first
    second = rest.astype(BF16).astype(F32)
    return first, second, rest - second


def partner(axis, which):
    index = lax.axis_index(axis)
    step = 1 - 2 * lax.rem(index, 2)
    if which:
        step = -step
    there = index + step
    return step, (there >= 0) & (there < lax.axis_size(axis))


def swap(block, axis, which):
    count = lax.axis_size(axis)
    pairs = [(i, i + 1) for i in range(which, count - 1, 2)]
    return lax.ppermute(block, axis, pairs + [(b, a) for a, b in pairs])


def features(block, step_x, step_y, present, half_depth):
    row = lax.broadcasted_iota(jnp.int32, block.shape, 0)
    scale = jnp.where(row == 2, 2.0 * half_depth * PAIR_SCALE, PAIR_SCALE)
    shift = jnp.where(
        row == 0,
        (step_x.astype(F32) - 0.5) * PAIR_SCALE,
        jnp.where(row == 1, (step_y.astype(F32) - 0.5) * PAIR_SCALE, -half_depth * PAIR_SCALE),
    )
    place = jnp.where(row < 3, block * scale + shift, 0.0)
    norm = -0.5 * jnp.sum(place * place, axis=0, keepdims=True)
    norm = jnp.where(present, norm, NEVER)
    source = jnp.where(row == 3, norm, jnp.where(row == 4, 1.0, place))
    target = jnp.where(row == 3, 1.0, jnp.where(row == 4, norm, place))
    return place, source, target


def target_rows(own, half_depth):
    place, _, target = features(own, jnp.int32(0), jnp.int32(0), True, half_depth)
    a, b, c = split3(target)
    return place, jnp.concatenate([a, b, a, b, c, a], axis=0).astype(BF16)


def depth_centres(depth):
    return (lax.broadcasted_iota(jnp.int32, (1, depth), 1).astype(F32) + 0.5) * FILTER_SCALE


def depth_column(block, depth):
    return jnp.transpose(block[0:8] * (depth * FILTER_SCALE))[:, 2:3]


def depth_rows(column, depth):
    distance = column - depth_centres(depth)
    bumps = jnp.exp2(-(distance * distance))
    return (bumps * (1.0 / jnp.sum(bumps, axis=1, keepdims=True))).astype(BF16)


def pair_block(block, step_x, step_y, present, half_depth, target_ref, total_ref, depth_ref):
    particles = block.shape[1]
    depth = depth_ref.shape[1]
    column = depth_column(block, depth)
    _, source, _ = features(block, step_x, step_y, present, half_depth)
    a, b, c = split3(source)
    rows = jnp.concatenate([a, a, b, b, a, c], axis=0).astype(BF16)
    row = lax.broadcasted_iota(jnp.int32, a.shape, 0)
    moved = jnp.where(row < 7, pltpu.roll(b, 4, 0), 0.0)
    first = jnp.where(row < 3, a, jnp.where(row == 3, 1.0, moved))
    values = jnp.concatenate([first, jnp.where(row < 3, c, 0.0)], axis=0).astype(BF16)
    width = min(256, particles)
    for start in range(0, particles, width):
        exponent = lax.dot_general(
            rows,
            target_ref[:, start : start + width],
            (((0,), (0,)), ((), ())),
            preferred_element_type=F32,
        )
        weight = jnp.exp2(exponent)
        high = weight.astype(BF16)
        low = (weight - high.astype(F32)).astype(BF16)
        sums = jnp.dot(values, high, preferred_element_type=F32) + jnp.dot(
            values, low, preferred_element_type=F32
        )
        total_ref[:, start : start + width] += sums
        depth_ref[start : start + width] = depth_rows(column[start : start + width], depth)


def y_steps():
    step_a, has_a = partner("gy", 0)
    step_b, has_b = partner("gy", 1)
    return ((step_a, has_a), (jnp.int32(0), jnp.bool_(True)), (step_b, has_b))


def interpolate(request, table_ref, basis_ref, weight_ref):
    slots = request.shape[1]
    elements = table_ref.shape[0] // 6
    level = lax.broadcasted_iota(jnp.int32, (QUANT, slots), 0).astype(F32)
    factors = []
    for axis in range(3):
        chosen = jnp.where(level == request[1 + axis : 2 + axis], 1.0, 0.0).astype(BF16)
        parts = jnp.dot(basis_ref[...], chosen, preferred_element_type=F32)
        factors.append(parts[0:8] + (parts[8:16] + parts[16:24]))
    for a in range(NODES):
        first = factors[0][a : a + 1] * factors[1]
        for b in range(0, NODES, 2):
            pair = jnp.concatenate(
                [first[b : b + 1] * factors[2], first[b + 1 : b + 2] * factors[2]], axis=0
            )
            start = (a * NODES + b) * NODES
            weight_ref[start : start + 2 * NODES, :slots] = pair.astype(BF16)
    projected = jnp.dot(table_ref[...], weight_ref[:, :slots], preferred_element_type=F32)
    local = lax.broadcasted_iota(jnp.int32, (elements, slots), 0).astype(F32)
    picked = jnp.where(local == request[0:1], 1.0, 0.0)
    rows = [
        jnp.sum(projected[k * elements : (k + 1) * elements] * picked, axis=0, keepdims=True)
        for k in range(6)
    ]
    return jnp.concatenate(rows + [jnp.zeros((2, slots), F32)], axis=0)


def my_flat():
    return (lax.axis_index("gx") * lax.axis_size("gy") + lax.axis_index("gy")).astype(F32)


def fetch_all(sources, targets, arrived):
    fetches = [
        pltpu.make_async_copy(source, target, arrived.at[n])
        for n, (source, target) in enumerate(zip(sources, targets))
    ]
    for fetch in fetches:
        fetch.start()
    return fetches


def pack_kernel(
    far_fractions_ref, far_owner_ref, far_element_ref, far_coords_ref, out_ref,
    fractions_ref, owner_ref, element_ref, coords_ref, arrived,
):
    for fetch in fetch_all(
        (far_fractions_ref, far_owner_ref, far_element_ref, far_coords_ref),
        (fractions_ref, owner_ref, element_ref, coords_ref),
        arrived,
    ):
        fetch.wait()
    for k in range(3):
        out_ref[k : k + 1] = fractions_ref[k]
        out_ref[5 + k : 6 + k] = coords_ref[k].astype(F32)
    out_ref[3:4] = owner_ref[...].astype(F32)
    out_ref[4:5] = element_ref[...].astype(F32)


def own_kernel(
    half_depth, own_ref, far_table_ref, far_basis_ref, total_ref, values_ref, depth_ref,
    target_ref, weight_ref, table_ref, basis_ref, arrived,
):
    fetches = fetch_all((far_table_ref, far_basis_ref), (table_ref, basis_ref), arrived)
    own = own_ref[...]
    _, target = target_rows(own, half_depth)
    target_ref[...] = target
    total_ref[...] = jnp.zeros_like(total_ref)
    zero = jnp.int32(0)
    pair_block(own, zero, zero, True, half_depth, target_ref, total_ref, depth_ref)
    for fetch in fetches:
        fetch.wait()
    values = interpolate(own[4:8], table_ref, basis_ref, weight_ref)
    values_ref[...] = jnp.where(own[3:4] == my_flat(), values, 0.0).astype(BF16)


def column_kernel(
    half_depth, own_ref, first_ref, second_ref, sum_ref, total_ref, depth_ref, target_ref
):
    _, target = target_rows(own_ref[...], half_depth)
    target_ref[...] = target
    total_ref[...] = sum_ref[...]
    steps = y_steps()
    zero = jnp.int32(0)
    for n, (ref, (step, present)) in enumerate(((first_ref, steps[0]), (second_ref, steps[2]))):
        pair_block(ref[...], zero, step, present, half_depth, target_ref, total_ref, depth_ref.at[n])


def side_kernel(
    which, half_depth, own_ref, blocks_ref, sum_ref, total_ref, depth_ref, target_ref
):
    _, target = target_rows(own_ref[...], half_depth)
    target_ref[...] = target
    total_ref[...] = sum_ref[...]
    step_x, has_x = partner("gx", which)
    for k, (step, present) in enumerate(y_steps()):
        pair_block(
            blocks_ref[k], step_x, step, present & has_x, half_depth, target_ref, total_ref,
            depth_ref.at[k],
        )


def serve_kernel(
    za_ref, zb_ref, xa_ref, xb_ref, table_ref, basis_ref,
    zout_ref, xaout_ref, xbout_ref, chosen_ref, weight_ref,
):
    particles = za_ref.shape[1]
    steps = y_steps()
    _, has_a = partner("gx", 0)
    _, has_b = partner("gx", 1)
    blocks = [(za_ref[...], steps[0][1], (zout_ref, 0)), (zb_ref[...], steps[2][1], (zout_ref, 1))]
    for ref, out, has in ((xa_ref, xaout_ref, has_a), (xb_ref, xbout_ref, has_b)):
        for k in range(3):
            blocks.append((ref[k], steps[k][1] & has, (out, k)))
    me = my_flat()
    mask = jnp.concatenate(
        [jnp.where((b[3:4] == me) & present, 1.0, 0.0) for b, present, _ in blocks], axis=0
    )
    lanes = 128
    chunks = particles // lanes
    upper = jnp.where(
        lax.broadcasted_iota(jnp.int32, (lanes, lanes), 0)
        < lax.broadcasted_iota(jnp.int32, (lanes, lanes), 1),
        1.0,
        0.0,
    ).astype(BF16)
    stacked = jnp.concatenate([mask[:, j * lanes : (j + 1) * lanes] for j in range(chunks)], axis=0)
    inside = jnp.dot(stacked.astype(BF16), upper, preferred_element_type=F32)
    counts = jnp.sum(stacked, axis=1, keepdims=True)
    before = jnp.zeros((8, 1), F32)
    ranks = []
    for j in range(chunks):
        ranks.append(inside[8 * j : 8 * j + 8] + before)
        before = before + counts[8 * j : 8 * j + 8]
    rank = jnp.concatenate(ranks, axis=1)
    slot = lax.broadcasted_iota(jnp.int32, (2 * CAP, particles), 0).astype(F32)
    requests = []
    for pair in range(4):
        part = jnp.zeros((8, 2 * CAP), F32)
        for half in range(2):
            b = 2 * pair + half
            place = jnp.where(mask[b : b + 1] > 0.0, rank[b : b + 1] + half * CAP, -1.0)
            chosen = jnp.where(slot == place, 1.0, 0.0).astype(BF16)
            chosen_ref[b] = chosen
            part = part + lax.dot_general(
                blocks[b][0].astype(BF16), chosen, (((1,), (1,)), ((), ())), preferred_element_type=F32
            )
        requests.append(part)
    request = jnp.concatenate(requests, axis=1)
    values = interpolate(request[4:8], table_ref, basis_ref, weight_ref).astype(BF16)
    for b, (_, _, (out, k)) in enumerate(blocks):
        reply = values[:, (b // 2) * 2 * CAP : (b // 2 + 1) * 2 * CAP]
        out[k] = jnp.dot(reply, chosen_ref[b], preferred_element_type=F32).astype(BF16)


def join_kernel(own_ref, z_ref, xa_ref, xb_ref, mid_ref, za_ref, zb_ref):
    za_ref[...] = z_ref[0] + (xa_ref[0] + xb_ref[0])
    mid_ref[...] = own_ref[...] + (xa_ref[1] + xb_ref[1])
    zb_ref[...] = z_ref[1] + (xa_ref[2] + xb_ref[2])


def force_kernel(
    half_depth, own_ref, mid_ref, za_ref, zb_ref, total_ref, velocity_ref, drag_ref, volume_ref,
    force_ref, loads_ref,
):
    place, _, _ = features(own_ref[...], jnp.int32(0), jnp.int32(0), True, half_depth)
    total = total_ref[...]
    first = total[0:3] + (total[4:7] + total[8:11])
    pair = (STIFFNESS / PAIR_SCALE) * (place[0:3] * total[3:4] - first)
    fetched = (mid_ref[...] + (za_ref[...] + zb_ref[...])).astype(F32)
    for k in range(3):
        force = (
            drag_ref[...] * (fetched[k : k + 1] - velocity_ref[k])
            - volume_ref[...] * fetched[3 + k : 4 + k]
            + pair[k : k + 1]
        )
        force_ref[k] = force
        loads_ref[k : k + 1] = force
    loads_ref[3:4] = volume_ref[...]


def side_weights(fraction_row, bins, first, count, rows, low):
    particles = fraction_row.shape[1]
    extent = bins + 2 * MARGIN
    along = fraction_row * (bins * FILTER_SCALE)
    index = lax.broadcasted_iota(jnp.int32, (extent, particles), 0).astype(F32)
    distance = along - (index - (MARGIN - 0.5)) * FILTER_SCALE
    inverse = 1.0 / jnp.sum(jnp.exp2(-(distance * distance)), axis=0, keepdims=True)
    row = lax.broadcasted_iota(jnp.int32, (rows, particles), 0)
    here = row.astype(F32) + first.astype(F32)
    distance = along - (here - (MARGIN - 0.5)) * FILTER_SCALE
    bumps = jnp.exp2(-(distance * distance)) * inverse
    return jnp.where((row >= low) & (row < low + count), bumps, 0.0)


def cross_axis(step, bins):
    return jnp.where(step < 0, bins + MARGIN, 0), jnp.where(step < 0, 0, bins - MARGIN)


def x_part(block, step):
    first, to = cross_axis(step, BX)
    return side_weights(block[0:1], BX, first, MARGIN, 8, 0), to


def y_part(block, step):
    first, _ = cross_axis(step, BY)
    low = jnp.where(step < 0, 0, MARGIN)
    return side_weights(block[1:2], BY, first - low, MARGIN, 8, low), jnp.where(step < 0, 0, BY - 8)


def whole_part(row, bins):
    return side_weights(row, bins, jnp.int32(MARGIN), bins, bins, 0)


def spread_rows(along_x, count_x, along_y, load, spread_ref):
    rows = along_y.shape[0]
    group = max(1, 16 // rows)
    for a in range(0, count_x, group):
        parts = [(along_x[a + i : a + i + 1] * along_y) * load for i in range(group)]
        part = parts[0] if group == 1 else jnp.concatenate(parts, axis=0)
        spread_ref[a * rows : (a + group) * rows] = part.astype(BF16)


def spread_product(along_x, count_x, along_y, load, depth, spread_ref):
    rows = along_y.shape[0]
    spread_rows(along_x, count_x, along_y, load, spread_ref)
    piece = jnp.dot(spread_ref[: count_x * rows], depth, preferred_element_type=F32)
    return piece.reshape(count_x, rows, piece.shape[1])


def filter_own_kernel(scale, own_ref, loads_ref, depth_ref, out_ref, spread_ref):
    own = own_ref[...]
    depth = depth_ref[...]
    along_x = whole_part(own[0:1], BX)
    along_y = whole_part(own[1:2], BY)
    for c in range(4):
        out_ref[c] = spread_product(
            along_x, BX, along_y, loads_ref[c : c + 1] * scale, depth, spread_ref
        )


def planes_into(ref, along_x, count_x, along_y):
    rows = along_y.shape[0]
    for a in range(count_x):
        ref[a * rows : (a + 1) * rows] = along_x[a : a + 1] * along_y


def scatter_loads(plane, loads, scale, spread_ref):
    rows = plane.shape[0]
    count = loads.shape[0]
    for c in range(count):
        spread_ref[c * rows : (c + 1) * rows] = (plane * (loads[c : c + 1] * scale)).astype(BF16)
    return spread_ref[: count * rows]


def filter_x_kernel(
    scale, xa_ref, xb_ref, za_ref, zb_ref, la_ref, lb_ref, da_ref, db_ref,
    out_ref, mid_ref, corner_ref, plane_ref, spread_ref,
):
    depth = out_ref.shape[4]
    y_offsets = (y_steps()[0][0], y_steps()[2][0])
    for which, (ref, loads, depth_ref) in enumerate(
        ((xa_ref, la_ref, da_ref), (xb_ref, lb_ref, db_ref))
    ):
        step, _ = partner("gx", which)
        block = ref[1]
        planes_into(plane_ref, x_part(block, step)[0], MARGIN, whole_part(block[1:2], BY))
        spread = scatter_loads(plane_ref[...], loads[...], scale, spread_ref)
        piece = jnp.dot(spread, depth_ref[1], preferred_element_type=F32)
        out_ref[which] = piece.reshape(4, MARGIN, BY, depth)
        for side in range(2):
            block = ref[2 * side]
            along_y = y_part(block, y_offsets[side])[0]
            planes_into(corner_ref.at[2 * side + which], x_part(block, step)[0], MARGIN, along_y)
    for side, ref in enumerate((za_ref, zb_ref)):
        block = ref[...]
        along_y = y_part(block, y_offsets[side])[0]
        planes_into(mid_ref.at[side], whole_part(block[0:1], BX), BX, along_y)


def filter_rest_kernel(
    scale, mid_ref, corner_ref, la_ref, lb_ref, dz_ref, da_ref, db_ref, side_ref, field_ref,
    out_ref, sum_ref, spread_ref, sent,
):
    depth = out_ref.shape[3]
    y_offsets = (y_steps()[0][0], y_steps()[2][0])
    copies = []
    for side, loads in enumerate((la_ref, lb_ref)):
        half = pl.ds(pl.multiple_of(jnp.where(y_offsets[side] < 0, 0, BY - 8), 8), 8)
        sum_ref[side] = field_ref[:, :, half]
        for which, depth_ref in enumerate((da_ref, db_ref)):
            to_x = pl.ds(cross_axis(partner("gx", which)[0], BX)[1], MARGIN)
            plane = corner_ref[2 * side + which]
            spread = scatter_loads(plane, loads[2 * which], scale, spread_ref)
            piece = jnp.dot(spread, depth_ref[2 * side], preferred_element_type=F32)
            sum_ref[side, :, to_x] += (
                piece.reshape(4, MARGIN, 8, depth) + side_ref[which, :, :, half]
            )
        for c in range(0, 4, 2):
            spread = scatter_loads(mid_ref[side], loads[1, c : c + 2], scale, spread_ref)
            piece = jnp.dot(spread, dz_ref[side], preferred_element_type=F32)
            sum_ref[side, c : c + 2] += piece.reshape(2, BX, 8, depth)
            copy = pltpu.make_async_copy(
                sum_ref.at[side, c : c + 2], out_ref.at[c : c + 2, :, half], sent.at[len(copies)]
            )
            copy.start()
            copies.append(copy)
    for copy in copies:
        copy.wait()


def far(array):
    return pltpu.with_memory_space_constraint(array, pltpu.HBM)


def call(kernel, shapes, args, scratch=(), flops=0, name=None, mib=12, far=(), far_out=False):
    many = isinstance(shapes, list)
    return pl.pallas_call(
        kernel,
        out_shape=shapes,
        in_specs=[
            pl.BlockSpec(memory_space=pltpu.HBM) if i in far else VMEM for i in range(len(args))
        ],
        out_specs=[VMEM] * len(shapes)
        if many
        else pl.BlockSpec(memory_space=pltpu.HBM)
        if far_out
        else VMEM,
        scratch_shapes=list(scratch),
        cost_estimate=pl.CostEstimate(flops=flops, bytes_accessed=1 << 16, transcendentals=0),
        compiler_params=pltpu.CompilerParams(vmem_limit_bytes=mib << 20),
        name=name,
    )(*args)


def body(fractions, velocity, drag_rate, volume, owner, element, coords, fluid):
    particles = fractions.shape[3]
    elements = fluid.shape[2]
    depth = 512
    half_depth = 0.5 * depth / BX
    table = fluid.reshape(elements, 6, fluid.shape[4]).transpose(1, 0, 2)
    table = table.reshape(6 * elements, fluid.shape[4])
    basis = jnp.asarray(split_table())
    row = (1, particles)
    planes = (3, 1, particles)
    block = jax.ShapeDtypeStruct((8, particles), F32)
    reply = jax.ShapeDtypeStruct((8, particles), BF16)
    sums = jax.ShapeDtypeStruct((16, particles), F32)
    target = pltpu.VMEM((48, particles), BF16)
    weights = pltpu.VMEM((fluid.shape[4], max(particles, 8 * CAP)), BF16)
    cost = particles * particles * 1000

    own = call(
        pack_kernel,
        block,
        tuple(
            far(x)
            for x in (
                fractions.reshape(planes),
                owner.reshape(row),
                element.reshape(row),
                coords.reshape(planes),
            )
        ),
        (
            pltpu.VMEM(planes, F32),
            pltpu.VMEM(row, jnp.int32),
            pltpu.VMEM(row, jnp.int32),
            pltpu.VMEM(planes, jnp.int32),
            pltpu.SemaphoreType.DMA((4,)),
        ),
        flops=1000,
        name="pack",
        mib=4,
        far=(0, 1, 2, 3),
    )
    zb = swap(own, "gy", 1)
    za = swap(own, "gy", 0)
    def depths(*lead):
        return jax.ShapeDtypeStruct((*lead, particles, depth), BF16)

    total, values, d_own = call(
        partial(own_kernel, half_depth),
        [sums, reply, depths()],
        (own, far(table), far(basis)),
        (target, weights, pltpu.VMEM(table.shape, BF16), pltpu.VMEM(basis.shape, BF16), pltpu.SemaphoreType.DMA((2,))),
        flops=2 * cost,
        name="own",
        far=(1, 2),
    )
    column = jnp.stack([za, own, zb])
    xb = swap(column, "gx", 1)
    xa = swap(column, "gx", 0)
    total, d_z = call(
        partial(column_kernel, half_depth),
        [sums, depths(2)],
        (own, za, zb, total),
        (target,),
        flops=2 * cost,
        name="column",
    )
    reply3 = jax.ShapeDtypeStruct((3, 8, particles), BF16)
    reply2 = jax.ShapeDtypeStruct((2, 8, particles), BF16)
    z_out, xa_out, xb_out = call(
        serve_kernel,
        [reply2, reply3, reply3],
        (za, zb, xa, xb, table, basis),
        (pltpu.VMEM((8, 2 * CAP, particles), BF16), weights),
        flops=2 * cost,
        name="serve",
        mib=12,
    )
    xb_in = swap(xb_out, "gx", 1)
    xa_in = swap(xa_out, "gx", 0)
    total, d_a = call(
        partial(side_kernel, 0, half_depth),
        [sums, depths(3)],
        (own, xa, total),
        (target,),
        flops=3 * cost,
        name="side_a",
    )
    mid, za_out, zb_out = call(
        join_kernel, [reply] * 3, (values, z_out, xa_in, xb_in), flops=1000, name="join"
    )
    zb_in = swap(zb_out, "gy", 1)
    za_in = swap(za_out, "gy", 0)
    total, d_b = call(
        partial(side_kernel, 1, half_depth),
        [sums, depths(3)],
        (own, xb, total),
        (target,),
        flops=3 * cost,
        name="side_b",
    )
    force, loads = call(
        partial(force_kernel, half_depth),
        [jax.ShapeDtypeStruct(planes, F32), jax.ShapeDtypeStruct((4, particles), F32)],
        (
            own,
            mid,
            za_in,
            zb_in,
            total,
            velocity.reshape(planes),
            drag_rate.reshape(row),
            volume.reshape(row),
        ),
        flops=1000,
        name="force",
    )
    lb = swap(loads, "gx", 1)
    la = swap(loads, "gx", 0)
    scale = BX * BY * depth / particles
    spread = pltpu.VMEM((BX * BY, particles), BF16)
    field = call(
        partial(filter_own_kernel, scale),
        jax.ShapeDtypeStruct((4, BX, BY, depth), F32),
        (own, loads, d_own),
        (spread,),
        flops=2 * cost,
        name="filter_own",
        mib=16,
    )
    load_row = jnp.stack([la, loads, lb])
    lzb = swap(load_row, "gy", 1)
    lza = swap(load_row, "gy", 0)
    sides, mids, corners = call(
        partial(filter_x_kernel, scale),
        [
            jax.ShapeDtypeStruct((2, 4, MARGIN, BY, depth), F32),
            jax.ShapeDtypeStruct((2, BX * 8, particles), F32),
            jax.ShapeDtypeStruct((4, MARGIN * 8, particles), F32),
        ],
        (xa, xb, za, zb, la, lb, d_a, d_b),
        (pltpu.VMEM((MARGIN * BY, particles), F32), spread),
        flops=2 * cost,
        name="filter_x",
        mib=16,
    )
    field = call(
        partial(filter_rest_kernel, scale),
        jax.ShapeDtypeStruct((4, BX, BY, depth), F32),
        (mids, corners, lza, lzb, d_z, d_a, d_b, sides, field),
        (
            pltpu.VMEM((2, 4, BX, 8, depth), F32),
            spread,
            pltpu.SemaphoreType.DMA((4,)),
        ),
        flops=4 * cost,
        name="filter_rest",
        mib=16,
        far_out=True,
    )
    return (force.reshape(1, 1, 3, particles), field)


def solution(mesh):
    return jax.shard_map(
        body,
        mesh=mesh,
        in_specs=(
            P("gx", "gy", None, None),
            P("gx", "gy", None, None),
            P("gx", "gy", None),
            P("gx", "gy", None),
            P("gx", "gy", None, None),
            P("gx", "gy", None),
            P("gx", "gy", None, None),
            P("gx", "gy", None, None, None),
        ),
        out_specs=(P("gx", "gy", None, None), P(None, "gx", "gy", None)),
        check_vma=False,
    )
```

```python
import math
from functools import partial

import jax
import jax.numpy as jnp
import numpy as np
from jax import lax
from jax.experimental import pallas as pl
from jax.experimental.pallas import tpu as pltpu
from jax.sharding import PartitionSpec as P


BX = 16
BY = 16
MARGIN = 4
QUANT = 64
CAP = 64
NODES = 8

GLL_NODES = (
    -1.0,
    -0.8717401485096066,
    -0.5917001814331423,
    -0.2092992179024789,
    0.2092992179024789,
    0.5917001814331423,
    0.8717401485096066,
    1.0,
)
STIFFNESS = 0.5
PAIR_WIDTH = 0.3
FILTER_BINS = 3.0

F32 = jnp.float32
BF16 = jnp.bfloat16
VMEM = pl.BlockSpec(memory_space=pltpu.VMEM)
PAIR_SCALE = math.sqrt(math.log2(math.e)) / PAIR_WIDTH
FILTER_SCALE = math.sqrt(0.5 * math.log2(math.e)) / FILTER_BINS
NEVER = -1e30


def basis_table(levels):
    points = -1.0 + (2.0 * np.arange(levels) + 1.0) / levels
    lagrange = np.ones((levels, NODES))
    for node_a in range(NODES):
        for node_b in range(NODES):
            if node_b != node_a:
                lagrange[:, node_a] *= (points - GLL_NODES[node_b]) / (
                    GLL_NODES[node_a] - GLL_NODES[node_b]
                )
    return lagrange.astype(np.float32)


def split_table():
    table = basis_table(QUANT).T
    parts = []
    for _ in range(3):
        head = table.astype(jnp.bfloat16)
        parts.append(head)
        table = table - head.astype(np.float32)
    return np.concatenate(parts, axis=0)


def split3(values):
    first = values.astype(BF16).astype(F32)
    rest = values - first
    second = rest.astype(BF16).astype(F32)
    return first, second, rest - second


def partner(axis, which):
    index = lax.axis_index(axis)
    step = 1 - 2 * lax.rem(index, 2)
    if which:
        step = -step
    there = index + step
    return step, (there >= 0) & (there < lax.axis_size(axis))


def swap(block, axis, which):
    count = lax.axis_size(axis)
    pairs = [(i, i + 1) for i in range(which, count - 1, 2)]
    return lax.ppermute(block, axis, pairs + [(b, a) for a, b in pairs])


def features(block, step_x, step_y, present, half_depth):
    row = lax.broadcasted_iota(jnp.int32, block.shape, 0)
    scale = jnp.where(row == 2, 2.0 * half_depth * PAIR_SCALE, PAIR_SCALE)
    shift = jnp.where(
        row == 0,
        (step_x.astype(F32) - 0.5) * PAIR_SCALE,
        jnp.where(row == 1, (step_y.astype(F32) - 0.5) * PAIR_SCALE, -half_depth * PAIR_SCALE),
    )
    place = jnp.where(row < 3, block * scale + shift, 0.0)
    norm = -0.5 * jnp.sum(place * place, axis=0, keepdims=True)
    norm = jnp.where(present, norm, NEVER)
    source = jnp.where(row == 3, norm, jnp.where(row == 4, 1.0, place))
    target = jnp.where(row == 3, 1.0, jnp.where(row == 4, norm, place))
    return place, source, target


def target_rows(own, half_depth):
    place, _, target = features(own, jnp.int32(0), jnp.int32(0), True, half_depth)
    a, b, c = split3(target)
    return place, jnp.concatenate([a, b, a, b, c, a], axis=0).astype(BF16)


def depth_centres(depth):
    return (lax.broadcasted_iota(jnp.int32, (1, depth), 1).astype(F32) + 0.5) * FILTER_SCALE


def depth_column(block, depth):
    return jnp.transpose(block[0:8] * (depth * FILTER_SCALE))[:, 2:3]


def depth_rows(column, depth):
    distance = column - depth_centres(depth)
    bumps = jnp.exp2(-(distance * distance))
    return (bumps * (1.0 / jnp.sum(bumps, axis=1, keepdims=True))).astype(BF16)


def pair_block(block, step_x, step_y, present, half_depth, target_ref, total_ref, depth_ref):
    particles = block.shape[1]
    depth = depth_ref.shape[1]
    column = depth_column(block, depth)
    _, source, _ = features(block, step_x, step_y, present, half_depth)
    a, b, c = split3(source)
    rows = jnp.concatenate([a, a, b, b, a, c], axis=0).astype(BF16)
    row = lax.broadcasted_iota(jnp.int32, a.shape, 0)
    moved = jnp.where(row < 7, pltpu.roll(b, 4, 0), 0.0)
    first = jnp.where(row < 3, a, jnp.where(row == 3, 1.0, moved))
    values = jnp.concatenate([first, jnp.where(row < 3, c, 0.0)], axis=0).astype(BF16)
    width = min(256, particles)
    for start in range(0, particles, width):
        exponent = lax.dot_general(
            rows,
            target_ref[:, start : start + width],
            (((0,), (0,)), ((), ())),
            preferred_element_type=F32,
        )
        weight = jnp.exp2(exponent)
        high = weight.astype(BF16)
        low = (weight - high.astype(F32)).astype(BF16)
        sums = jnp.dot(values, high, preferred_element_type=F32) + jnp.dot(
            values, low, preferred_element_type=F32
        )
        total_ref[:, start : start + width] += sums
        depth_ref[start : start + width] = depth_rows(column[start : start + width], depth)


def y_steps():
    step_a, has_a = partner("gy", 0)
    step_b, has_b = partner("gy", 1)
    return ((step_a, has_a), (jnp.int32(0), jnp.bool_(True)), (step_b, has_b))


def interpolate(request, table_ref, basis_ref, weight_ref):
    slots = request.shape[1]
    elements = table_ref.shape[0] // 6
    level = lax.broadcasted_iota(jnp.int32, (QUANT, slots), 0).astype(F32)
    factors = []
    for axis in range(3):
        chosen = jnp.where(level == request[1 + axis : 2 + axis], 1.0, 0.0).astype(BF16)
        parts = jnp.dot(basis_ref[...], chosen, preferred_element_type=F32)
        factors.append(parts[0:8] + (parts[8:16] + parts[16:24]))
    for a in range(NODES):
        first = factors[0][a : a + 1] * factors[1]
        for b in range(0, NODES, 2):
            pair = jnp.concatenate(
                [first[b : b + 1] * factors[2], first[b + 1 : b + 2] * factors[2]], axis=0
            )
            start = (a * NODES + b) * NODES
            weight_ref[start : start + 2 * NODES, :slots] = pair.astype(BF16)
    projected = jnp.dot(table_ref[...], weight_ref[:, :slots], preferred_element_type=F32)
    local = lax.broadcasted_iota(jnp.int32, (elements, slots), 0).astype(F32)
    picked = jnp.where(local == request[0:1], 1.0, 0.0)
    rows = [
        jnp.sum(projected[k * elements : (k + 1) * elements] * picked, axis=0, keepdims=True)
        for k in range(6)
    ]
    return jnp.concatenate(rows + [jnp.zeros((2, slots), F32)], axis=0)


def my_flat():
    return (lax.axis_index("gx") * lax.axis_size("gy") + lax.axis_index("gy")).astype(F32)


def fetch_all(sources, targets, arrived):
    fetches = [
        pltpu.make_async_copy(source, target, arrived.at[n])
        for n, (source, target) in enumerate(zip(sources, targets))
    ]
    for fetch in fetches:
        fetch.start()
    return fetches


def pack_kernel(
    far_fractions_ref, far_owner_ref, far_element_ref, far_coords_ref, out_ref,
    fractions_ref, owner_ref, element_ref, coords_ref, arrived,
):
    for fetch in fetch_all(
        (far_fractions_ref, far_owner_ref, far_element_ref, far_coords_ref),
        (fractions_ref, owner_ref, element_ref, coords_ref),
        arrived,
    ):
        fetch.wait()
    for k in range(3):
        out_ref[k : k + 1] = fractions_ref[k]
        out_ref[5 + k : 6 + k] = coords_ref[k].astype(F32)
    out_ref[3:4] = owner_ref[...].astype(F32)
    out_ref[4:5] = element_ref[...].astype(F32)


def own_kernel(
    half_depth, own_ref, far_table_ref, far_basis_ref, total_ref, values_ref, depth_ref,
    target_ref, weight_ref, table_ref, basis_ref, arrived,
):
    fetches = fetch_all((far_table_ref, far_basis_ref), (table_ref, basis_ref), arrived)
    own = own_ref[...]
    _, target = target_rows(own, half_depth)
    target_ref[...] = target
    total_ref[...] = jnp.zeros_like(total_ref)
    zero = jnp.int32(0)
    pair_block(own, zero, zero, True, half_depth, target_ref, total_ref, depth_ref)
    for fetch in fetches:
        fetch.wait()
    values = interpolate(own[4:8], table_ref, basis_ref, weight_ref)
    values_ref[...] = jnp.where(own[3:4] == my_flat(), values, 0.0).astype(BF16)


def column_kernel(
    half_depth, own_ref, first_ref, second_ref, sum_ref, total_ref, depth_ref, target_ref
):
    _, target = target_rows(own_ref[...], half_depth)
    target_ref[...] = target
    total_ref[...] = sum_ref[...]
    steps = y_steps()
    zero = jnp.int32(0)
    for n, (ref, (step, present)) in enumerate(((first_ref, steps[0]), (second_ref, steps[2]))):
        pair_block(ref[...], zero, step, present, half_depth, target_ref, total_ref, depth_ref.at[n])


def side_kernel(
    which, half_depth, own_ref, blocks_ref, sum_ref, total_ref, depth_ref, target_ref
):
    _, target = target_rows(own_ref[...], half_depth)
    target_ref[...] = target
    total_ref[...] = sum_ref[...]
    step_x, has_x = partner("gx", which)
    for k, (step, present) in enumerate(y_steps()):
        pair_block(
            blocks_ref[k], step_x, step, present & has_x, half_depth, target_ref, total_ref,
            depth_ref.at[k],
        )


def serve_kernel(
    za_ref, zb_ref, xa_ref, xb_ref, table_ref, basis_ref,
    zout_ref, xaout_ref, xbout_ref, chosen_ref, weight_ref,
):
    particles = za_ref.shape[1]
    steps = y_steps()
    _, has_a = partner("gx", 0)
    _, has_b = partner("gx", 1)
    blocks = [(za_ref[...], steps[0][1], (zout_ref, 0)), (zb_ref[...], steps[2][1], (zout_ref, 1))]
    for ref, out, has in ((xa_ref, xaout_ref, has_a), (xb_ref, xbout_ref, has_b)):
        for k in range(3):
            blocks.append((ref[k], steps[k][1] & has, (out, k)))
    me = my_flat()
    mask = jnp.concatenate(
        [jnp.where((b[3:4] == me) & present, 1.0, 0.0) for b, present, _ in blocks], axis=0
    )
    lanes = 128
    chunks = particles // lanes
    upper = jnp.where(
        lax.broadcasted_iota(jnp.int32, (lanes, lanes), 0)
        < lax.broadcasted_iota(jnp.int32, (lanes, lanes), 1),
        1.0,
        0.0,
    ).astype(BF16)
    stacked = jnp.concatenate([mask[:, j * lanes : (j + 1) * lanes] for j in range(chunks)], axis=0)
    inside = jnp.dot(stacked.astype(BF16), upper, preferred_element_type=F32)
    counts = jnp.sum(stacked, axis=1, keepdims=True)
    before = jnp.zeros((8, 1), F32)
    ranks = []
    for j in range(chunks):
        ranks.append(inside[8 * j : 8 * j + 8] + before)
        before = before + counts[8 * j : 8 * j + 8]
    rank = jnp.concatenate(ranks, axis=1)
    slot = lax.broadcasted_iota(jnp.int32, (2 * CAP, particles), 0).astype(F32)
    requests = []
    for pair in range(4):
        part = jnp.zeros((8, 2 * CAP), F32)
        for half in range(2):
            b = 2 * pair + half
            place = jnp.where(mask[b : b + 1] > 0.0, rank[b : b + 1] + half * CAP, -1.0)
            chosen = jnp.where(slot == place, 1.0, 0.0).astype(BF16)
            chosen_ref[b] = chosen
            part = part + lax.dot_general(
                blocks[b][0].astype(BF16), chosen, (((1,), (1,)), ((), ())), preferred_element_type=F32
            )
        requests.append(part)
    request = jnp.concatenate(requests, axis=1)
    values = interpolate(request[4:8], table_ref, basis_ref, weight_ref).astype(BF16)
    for b, (_, _, (out, k)) in enumerate(blocks):
        reply = values[:, (b // 2) * 2 * CAP : (b // 2 + 1) * 2 * CAP]
        out[k] = jnp.dot(reply, chosen_ref[b], preferred_element_type=F32).astype(BF16)


def join_kernel(own_ref, z_ref, xa_ref, xb_ref, mid_ref, za_ref, zb_ref):
    za_ref[...] = z_ref[0] + (xa_ref[0] + xb_ref[0])
    mid_ref[...] = own_ref[...] + (xa_ref[1] + xb_ref[1])
    zb_ref[...] = z_ref[1] + (xa_ref[2] + xb_ref[2])


def force_kernel(
    half_depth, own_ref, mid_ref, za_ref, zb_ref, total_ref, velocity_ref, drag_ref, volume_ref,
    force_ref, loads_ref,
):
    place, _, _ = features(own_ref[...], jnp.int32(0), jnp.int32(0), True, half_depth)
    total = total_ref[...]
    first = total[0:3] + (total[4:7] + total[8:11])
    pair = (STIFFNESS / PAIR_SCALE) * (place[0:3] * total[3:4] - first)
    fetched = (mid_ref[...] + (za_ref[...] + zb_ref[...])).astype(F32)
    for k in range(3):
        force = (
            drag_ref[...] * (fetched[k : k + 1] - velocity_ref[k])
            - volume_ref[...] * fetched[3 + k : 4 + k]
            + pair[k : k + 1]
        )
        force_ref[k] = force
        loads_ref[k : k + 1] = force
    loads_ref[3:4] = volume_ref[...]


def side_weights(fraction_row, bins, first, count, rows, low):
    particles = fraction_row.shape[1]
    extent = bins + 2 * MARGIN
    along = fraction_row * (bins * FILTER_SCALE)
    index = lax.broadcasted_iota(jnp.int32, (extent, particles), 0).astype(F32)
    distance = along - (index - (MARGIN - 0.5)) * FILTER_SCALE
    inverse = 1.0 / jnp.sum(jnp.exp2(-(distance * distance)), axis=0, keepdims=True)
    row = lax.broadcasted_iota(jnp.int32, (rows, particles), 0)
    here = row.astype(F32) + first.astype(F32)
    distance = along - (here - (MARGIN - 0.5)) * FILTER_SCALE
    bumps = jnp.exp2(-(distance * distance)) * inverse
    return jnp.where((row >= low) & (row < low + count), bumps, 0.0)


def cross_axis(step, bins):
    return jnp.where(step < 0, bins + MARGIN, 0), jnp.where(step < 0, 0, bins - MARGIN)


def x_part(block, step):
    first, to = cross_axis(step, BX)
    return side_weights(block[0:1], BX, first, MARGIN, 8, 0), to


def y_part(block, step):
    first, _ = cross_axis(step, BY)
    low = jnp.where(step < 0, 0, MARGIN)
    return side_weights(block[1:2], BY, first - low, MARGIN, 8, low), jnp.where(step < 0, 0, BY - 8)


def whole_part(row, bins):
    return side_weights(row, bins, jnp.int32(MARGIN), bins, bins, 0)


def spread_rows(along_x, count_x, along_y, load, spread_ref):
    rows = along_y.shape[0]
    group = max(1, 16 // rows)
    for a in range(0, count_x, group):
        parts = [(along_x[a + i : a + i + 1] * along_y) * load for i in range(group)]
        part = parts[0] if group == 1 else jnp.concatenate(parts, axis=0)
        spread_ref[a * rows : (a + group) * rows] = part.astype(BF16)


def spread_product(along_x, count_x, along_y, load, depth, spread_ref):
    rows = along_y.shape[0]
    spread_rows(along_x, count_x, along_y, load, spread_ref)
    piece = jnp.dot(spread_ref[: count_x * rows], depth, preferred_element_type=F32)
    return piece.reshape(count_x, rows, piece.shape[1])


def filter_own_kernel(scale, own_ref, loads_ref, depth_ref, out_ref, spread_ref):
    own = own_ref[...]
    depth = depth_ref[...]
    along_x = whole_part(own[0:1], BX)
    along_y = whole_part(own[1:2], BY)
    for c in range(4):
        out_ref[c] = spread_product(
            along_x, BX, along_y, loads_ref[c : c + 1] * scale, depth, spread_ref
        )


def planes_into(ref, along_x, count_x, along_y):
    rows = along_y.shape[0]
    for a in range(count_x):
        ref[a * rows : (a + 1) * rows] = along_x[a : a + 1] * along_y


def scatter_loads(plane, loads, scale, spread_ref):
    rows = plane.shape[0]
    count = loads.shape[0]
    for c in range(count):
        spread_ref[c * rows : (c + 1) * rows] = (plane * (loads[c : c + 1] * scale)).astype(BF16)
    return spread_ref[: count * rows]


def filter_x_kernel(
    scale, xa_ref, xb_ref, za_ref, zb_ref, la_ref, lb_ref, da_ref, db_ref,
    out_ref, mid_ref, corner_ref, plane_ref, spread_ref,
):
    depth = out_ref.shape[4]
    y_offsets = (y_steps()[0][0], y_steps()[2][0])
    for which, (ref, loads, depth_ref) in enumerate(
        ((xa_ref, la_ref, da_ref), (xb_ref, lb_ref, db_ref))
    ):
        step, _ = partner("gx", which)
        block = ref[1]
        planes_into(plane_ref, x_part(block, step)[0], MARGIN, whole_part(block[1:2], BY))
        spread = scatter_loads(plane_ref[...], loads[...], scale, spread_ref)
        piece = jnp.dot(spread, depth_ref[1], preferred_element_type=F32)
        out_ref[which] = piece.reshape(4, MARGIN, BY, depth)
        for side in range(2):
            block = ref[2 * side]
            along_y = y_part(block, y_offsets[side])[0]
            planes_into(corner_ref.at[2 * side + which], x_part(block, step)[0], MARGIN, along_y)
    for side, ref in enumerate((za_ref, zb_ref)):
        block = ref[...]
        along_y = y_part(block, y_offsets[side])[0]
        planes_into(mid_ref.at[side], whole_part(block[0:1], BX), BX, along_y)


def filter_rest_kernel(
    scale, mid_ref, corner_ref, la_ref, lb_ref, dz_ref, da_ref, db_ref, side_ref, field_ref,
    out_ref, sum_ref, spread_ref, sent,
):
    depth = out_ref.shape[3]
    y_offsets = (y_steps()[0][0], y_steps()[2][0])
    copies = []
    for side, loads in enumerate((la_ref, lb_ref)):
        half = pl.ds(pl.multiple_of(jnp.where(y_offsets[side] < 0, 0, BY - 8), 8), 8)
        sum_ref[side] = field_ref[:, :, half]
        for which, depth_ref in enumerate((da_ref, db_ref)):
            to_x = pl.ds(cross_axis(partner("gx", which)[0], BX)[1], MARGIN)
            plane = corner_ref[2 * side + which]
            spread = scatter_loads(plane, loads[2 * which], scale, spread_ref)
            piece = jnp.dot(spread, depth_ref[2 * side], preferred_element_type=F32)
            sum_ref[side, :, to_x] += (
                piece.reshape(4, MARGIN, 8, depth) + side_ref[which, :, :, half]
            )
        for c in range(0, 4, 2):
            spread = scatter_loads(mid_ref[side], loads[1, c : c + 2], scale, spread_ref)
            piece = jnp.dot(spread, dz_ref[side], preferred_element_type=F32)
            sum_ref[side, c : c + 2] += piece.reshape(2, BX, 8, depth)
            copy = pltpu.make_async_copy(
                sum_ref.at[side, c : c + 2], out_ref.at[c : c + 2, :, half], sent.at[len(copies)]
            )
            copy.start()
            copies.append(copy)
    for copy in copies:
        copy.wait()


def far(array):
    return pltpu.with_memory_space_constraint(array, pltpu.HBM)


def call(kernel, shapes, args, scratch=(), flops=0, mib=12, far=(), far_out=False):
    many = isinstance(shapes, list)
    return pl.pallas_call(
        kernel,
        out_shape=shapes,
        in_specs=[
            pl.BlockSpec(memory_space=pltpu.HBM) if i in far else VMEM for i in range(len(args))
        ],
        out_specs=[VMEM] * len(shapes)
        if many
        else pl.BlockSpec(memory_space=pltpu.HBM)
        if far_out
        else VMEM,
        scratch_shapes=list(scratch),
        cost_estimate=pl.CostEstimate(flops=flops, bytes_accessed=1 << 16, transcendentals=0),
        compiler_params=pltpu.CompilerParams(vmem_limit_bytes=mib << 20),
    )(*args)


def step(fractions, velocity, drag_rate, volume, owner, element, coords, fluid):
    particles = fractions.shape[3]
    elements = fluid.shape[2]
    depth = 512
    half_depth = 0.5 * depth / BX
    table = fluid.reshape(elements, 6, fluid.shape[4]).transpose(1, 0, 2)
    table = table.reshape(6 * elements, fluid.shape[4])
    basis = jnp.asarray(split_table())
    row = (1, particles)
    planes = (3, 1, particles)
    block = jax.ShapeDtypeStruct((8, particles), F32)
    reply = jax.ShapeDtypeStruct((8, particles), BF16)
    sums = jax.ShapeDtypeStruct((16, particles), F32)
    target = pltpu.VMEM((48, particles), BF16)
    weights = pltpu.VMEM((fluid.shape[4], max(particles, 8 * CAP)), BF16)
    cost = particles * particles * 1000

    own = call(
        pack_kernel,
        block,
        tuple(
            far(x)
            for x in (
                fractions.reshape(planes),
                owner.reshape(row),
                element.reshape(row),
                coords.reshape(planes),
            )
        ),
        (
            pltpu.VMEM(planes, F32),
            pltpu.VMEM(row, jnp.int32),
            pltpu.VMEM(row, jnp.int32),
            pltpu.VMEM(planes, jnp.int32),
            pltpu.SemaphoreType.DMA((4,)),
        ),
        flops=1000,
        mib=4,
        far=(0, 1, 2, 3),
    )
    zb = swap(own, "gy", 1)
    za = swap(own, "gy", 0)
    def depths(*lead):
        return jax.ShapeDtypeStruct((*lead, particles, depth), BF16)

    total, values, d_own = call(
        partial(own_kernel, half_depth),
        [sums, reply, depths()],
        (own, far(table), far(basis)),
        (target, weights, pltpu.VMEM(table.shape, BF16), pltpu.VMEM(basis.shape, BF16), pltpu.SemaphoreType.DMA((2,))),
        flops=2 * cost,
        far=(1, 2),
    )
    column = jnp.stack([za, own, zb])
    xb = swap(column, "gx", 1)
    xa = swap(column, "gx", 0)
    total, d_z = call(
        partial(column_kernel, half_depth),
        [sums, depths(2)],
        (own, za, zb, total),
        (target,),
        flops=2 * cost,
    )
    reply3 = jax.ShapeDtypeStruct((3, 8, particles), BF16)
    reply2 = jax.ShapeDtypeStruct((2, 8, particles), BF16)
    z_out, xa_out, xb_out = call(
        serve_kernel,
        [reply2, reply3, reply3],
        (za, zb, xa, xb, table, basis),
        (pltpu.VMEM((8, 2 * CAP, particles), BF16), weights),
        flops=2 * cost,
        mib=12,
    )
    xb_in = swap(xb_out, "gx", 1)
    xa_in = swap(xa_out, "gx", 0)
    total, d_a = call(
        partial(side_kernel, 0, half_depth),
        [sums, depths(3)],
        (own, xa, total),
        (target,),
        flops=3 * cost,
    )
    mid, za_out, zb_out = call(join_kernel, [reply] * 3, (values, z_out, xa_in, xb_in), flops=1000)
    zb_in = swap(zb_out, "gy", 1)
    za_in = swap(za_out, "gy", 0)
    total, d_b = call(
        partial(side_kernel, 1, half_depth),
        [sums, depths(3)],
        (own, xb, total),
        (target,),
        flops=3 * cost,
    )
    force, loads = call(
        partial(force_kernel, half_depth),
        [jax.ShapeDtypeStruct(planes, F32), jax.ShapeDtypeStruct((4, particles), F32)],
        (
            own,
            mid,
            za_in,
            zb_in,
            total,
            velocity.reshape(planes),
            drag_rate.reshape(row),
            volume.reshape(row),
        ),
        flops=1000,
    )
    lb = swap(loads, "gx", 1)
    la = swap(loads, "gx", 0)
    scale = BX * BY * depth / particles
    spread = pltpu.VMEM((BX * BY, particles), BF16)
    field = call(
        partial(filter_own_kernel, scale),
        jax.ShapeDtypeStruct((4, BX, BY, depth), F32),
        (own, loads, d_own),
        (spread,),
        flops=2 * cost,
        mib=16,
    )
    load_row = jnp.stack([la, loads, lb])
    lzb = swap(load_row, "gy", 1)
    lza = swap(load_row, "gy", 0)
    sides, mids, corners = call(
        partial(filter_x_kernel, scale),
        [
            jax.ShapeDtypeStruct((2, 4, MARGIN, BY, depth), F32),
            jax.ShapeDtypeStruct((2, BX * 8, particles), F32),
            jax.ShapeDtypeStruct((4, MARGIN * 8, particles), F32),
        ],
        (xa, xb, za, zb, la, lb, d_a, d_b),
        (pltpu.VMEM((MARGIN * BY, particles), F32), spread),
        flops=2 * cost,
        mib=16,
    )
    field = call(
        partial(filter_rest_kernel, scale),
        jax.ShapeDtypeStruct((4, BX, BY, depth), F32),
        (mids, corners, lza, lzb, d_z, d_a, d_b, sides, field),
        (
            pltpu.VMEM((2, 4, BX, 8, depth), F32),
            spread,
            pltpu.SemaphoreType.DMA((4,)),
        ),
        flops=4 * cost,
        mib=16,
        far_out=True,
    )
    return (force.reshape(1, 1, 3, particles), field)


def solution(mesh):
    return jax.shard_map(
        step,
        mesh=mesh,
        in_specs=(
            P("gx", "gy", None, None),
            P("gx", "gy", None, None),
            P("gx", "gy", None),
            P("gx", "gy", None),
            P("gx", "gy", None, None),
            P("gx", "gy", None),
            P("gx", "gy", None, None),
            P("gx", "gy", None, None, None),
        ),
        out_specs=(P("gx", "gy", None, None), P(None, "gx", "gy", None)),
        check_vma=False,
    )
```
